256 devices in a mesh: feat: 8 (over x, core), rows: 32 (over z, y).
Axes of the slice: x: 4, y: 4, z: 8, core: 2. Of those that a mesh axis runs over, the one named last changes fastest.
Arguments:
- features: bfloat16 [65536, 8192], P('rows', 'feat'), may hold values from -6 to 6
- residual: float32 [65536, 1024], P('rows', 'feat'), may hold values from -8 to 8
- inverse_grams: float32 [8192, 1024], P('feat'), may hold values from -1 to 1, as said below
Outputs:
- increments: bfloat16 [1024, 8192], P(None, 'feat')
- final_residual: float32 [65536, 1024], P('rows', 'feat')
The draws below stay inside these ranges and needn't reach their ends.
Inputs may be any that keep to these rules, and one draw needn't show every extreme that they name: `inverse_grams`: each block of 1024 rows is a symmetric positive definite matrix.
All inputs are finite; a program needn't handle non-finite values.
Results may differ from the reference program's by a relative error of at most 0.0051.
Values may be sent and summed in bfloat16 or wider, within the bound.
A program may use at most 64 MiB of HBM per device.

```python
import jax
import jax.numpy as jnp
from jax import lax

FB = 1024
LABELS = 1024
ROWS = 65536
NF = 8192
N_FEAT = 8


def draw_inverse_grams(key, part):
    count = NF // FB
    noise = jax.random.normal(key, (count, FB, FB), jnp.float32)
    symmetric = (noise + jnp.swapaxes(noise, 1, 2)) / jnp.sqrt(2.0 * FB)
    identity = jnp.eye(FB, dtype=jnp.float32)
    blocks_out = (identity[None, :, :] + 0.3 * symmetric) * (1.0 / ROWS)
    return blocks_out.reshape(NF, FB)


def block_levels(key, shape, shards, least, high):
    loudness = 1.0
    for axis_at, shards_of in shards:
        steps = jax.random.uniform(jax.random.fold_in(jax.random.fold_in(key, 6), axis_at), (shards_of,), jnp.float32, least / len(shards), high / len(shards))
        loudness = loudness * jnp.repeat(jnp.exp(steps), shape[axis_at] // shards_of).reshape((-1,) + (1,) * (len(shape) - 1 - axis_at))
    return loudness


def normal_values(own_key, shape, scale, most, pieces=(), kind=jnp.bfloat16):
    factor_of = block_levels(own_key, shape, pieces, -0.22, 0.18) if pieces else 1.0
    values = jax.random.normal(own_key, shape, jnp.float32) * scale * factor_of
    return jnp.minimum(jnp.maximum(values, -most), most).astype(kind)


def setup_inputs(seed: int = 0) -> dict:
    seeds = jax.random.split(jax.random.key(seed), 4)
    return {
        "features": normal_values(seeds[0], (ROWS, NF), 1.0, 6.0, ((0, 32), (1, 8))),
        "residual": normal_values(seeds[1], (ROWS, LABELS), 1.0, 8.0, ((0, 32), (1, 8)), jnp.float32),
        "inverse_grams": draw_inverse_grams(jax.random.fold_in(seeds[3], 71), 0),
    }


def reference(features, residual, inverse_grams):
    block_count = N_FEAT
    width = LABELS // block_count
    increments = jnp.zeros((LABELS, NF), jnp.bfloat16)
    finished = []
    for front in range(block_count):
        current = residual[:, front * width:(front + 1) * width]
        for visit in range(block_count):
            block = (front + visit) % block_count
            block_feats = features[:, block * FB:(block + 1) * FB]
            rounded = current.astype(jnp.bfloat16)
            projected = jnp.dot(rounded.T, block_feats, preferred_element_type=jnp.float32)
            inverse = inverse_grams[block * FB:(block + 1) * FB, :]
            update = jnp.dot(projected, inverse.T, precision=lax.Precision.HIGHEST).astype(jnp.bfloat16)
            current = current - jnp.dot(block_feats, update.T, preferred_element_type=jnp.float32)
            increments = increments.at[front * width:(front + 1) * width, block * FB:(block + 1) * FB].set(update)
        finished.append(current)
    return increments, jnp.concatenate(finished, axis=1)
```

```python
import functools

import jax
import jax.numpy as jnp
from jax import lax
from jax.experimental import pallas as pl
from jax.experimental.pallas import tpu as pltpu
from jax.sharding import PartitionSpec as P

NY = 4
CHAINS = 2
PIECES = 2
TILE = 256
MESH = pl.DeviceIdType.MESH
BF16, F32 = jnp.bfloat16, jnp.float32
NT = (((1,), (1,)), ((), ()))


def wait_for(ref, sem):
    pltpu.make_async_copy(ref, ref, sem).wait()


def sweep(nf, nz, x_hbm, r_hbm, h_hbm, inc_hbm, res_hbm, xv, yv, hst, hsp, rst, fin, inb, outb,
          acc, q, rb, yb, uall, x_in, h_in, r_in, x_recv, x_send, z_recv, z_send, y_recv, y_send,
          g_recv, g_send, out_sem):
    rows, fb = xv.shape
    width = acc.shape[1]
    cw = fb // nz
    kc = rows // PIECES
    visits = nf
    f = lax.axis_index("feat")
    rid = lax.axis_index("rows")
    z, y = rid // NY, rid % NY
    nxt, prv = (f + 1) % nf, (f + nf - 1) % nf

    def at_z(d):
        return {"rows": ((z + d) % nz) * NY + y}

    def at_y(d):
        return {"rows": z * NY + (y + d) % NY}

    z_order = sorted(range(1, nz), key=lambda d: -min(d, nz - d))
    x_blocks = rows // TILE

    def load_x(t):
        part = pl.ds(t * TILE, TILE)
        return pltpu.make_async_copy(x_hbm.at[part], xv.at[part], x_in.at[t])

    pltpu.make_async_copy(h_hbm, hst, h_in).start()
    pltpu.make_async_copy(r_hbm, rst, r_in).start()
    for t in range(x_blocks):
        load_x(t).start()

    barrier = pltpu.get_barrier_semaphore()
    for peer in [at_z(d) for d in range(1, nz)] + [at_y(d) for d in range(1, NY)] + [{"feat": nxt}, {"feat": prv}]:
        pl.semaphore_signal(barrier, inc=1, device_id=peer, device_id_type=MESH)

    pltpu.make_async_copy(h_hbm, hst, h_in).wait()

    @pl.loop(0, fb // 128)
    def _(i):
        part = pl.ds(pl.multiple_of(i * 128, 128), 128)
        value = hst[part, :]
        high = value.astype(BF16)
        hsp[0, part, :] = high
        hsp[1, part, :] = (value - high.astype(F32)).astype(BF16)

    pltpu.make_async_copy(r_hbm, rst, r_in).wait()

    @pl.loop(0, rows // 128)
    def _(i):
        part = pl.ds(pl.multiple_of(i * 128, 128), 128)
        value = rst[part, :].T
        high = value.astype(BF16)
        low = (value - high.astype(F32)).astype(BF16)
        for s in range(CHAINS):
            own = slice(s * width, (s + 1) * width)
            inb[0, s, 0, :, part] = high[own]
            inb[0, s, 1, :, part] = low[own]

    @pl.loop(0, x_blocks)
    def _(t):
        part = pl.ds(pl.multiple_of(t * TILE, TILE), TILE)
        pltpu.make_async_copy(x_hbm.at[part], xv.at[part], x_in.at[t]).wait()
        block = xv[part, :]
        for n in range(fb // TILE):
            cols = slice(n * TILE, (n + 1) * TILE)
            value = jnp.dot(block, hsp[0, :, cols], preferred_element_type=F32)
            value += jnp.dot(block, hsp[1, :, cols], preferred_element_type=F32)
            yv[part, cols] = value.astype(BF16)

    pl.semaphore_wait(barrier, nz - 1 + NY - 1 + 2)

    def project(v, s):
        for c in range(PIECES):
            part = slice(c * kc, (c + 1) * kc)

            @pl.when(v > 0)
            def _():
                wait_for(inb.at[v, s, 0, :, part], x_recv.at[v, s, c])

            high = inb[v, s, 0, :, part]
            for n in range(fb // TILE):
                cols = slice(n * TILE, (n + 1) * TILE)
                value = jnp.dot(high, yv[part, cols], preferred_element_type=F32)
                if c > 0:
                    value += acc[s, :, cols]
                if c < PIECES - 1:
                    acc[s, :, cols] = value
                else:
                    for i in range(TILE // cw):
                        q[s, n * (TILE // cw) + i] = value[:, i * cw:(i + 1) * cw].astype(BF16)
        for d in z_order:
            pltpu.make_async_remote_copy(
                q.at[s, (z + d) % nz], rb.at[v, s, d - 1], z_send.at[s], z_recv.at[v, s],
                device_id=at_z(d), device_id_type=MESH).start()

    def reduce_z(v, s):
        wait_for(rb.at[v, s], z_recv.at[v, s])
        total = q[s, z].astype(F32)
        for d in range(1, nz):
            total += rb[v, s, d - 1].astype(F32)
        yb[v, s, y] = total
        wait_for(rb.at[v, s], z_send.at[s])
        for d in (2, 1, 3):
            pltpu.make_async_remote_copy(
                yb.at[v, s, y], yb.at[v, s, y], y_send.at[s], y_recv.at[v, s],
                device_id=at_y(d), device_id_type=MESH).start()

    def reduce_y(v, s):
        wait_for(yb.at[v, s, pl.ds(0, NY - 1)], y_recv.at[v, s])
        wait_for(yb.at[v, s, pl.ds(0, NY - 1)], y_send.at[s])
        total = yb[v, s, 0] + yb[v, s, 1] + yb[v, s, 2] + yb[v, s, 3]
        front = (f - v + nf) % nf
        cols = pl.ds(pl.multiple_of(z * cw, cw), cw)
        row = front * CHAINS + s
        uall[row, :, cols] = total.astype(BF16)
        for d in z_order:
            pltpu.make_async_remote_copy(
                uall.at[row, :, cols], uall.at[row, :, cols], g_send.at[s], g_recv.at[v, s],
                device_id=at_z(d), device_id_type=MESH).start()

    def apply(v, s):
        front = (f - v + nf) % nf
        row = front * CHAINS + s
        wait_for(rb.at[v, s], g_recv.at[v, s])
        wait_for(rb.at[v, s], g_send.at[s])

        @pl.when(v > 0)
        def _():
            wait_for(inb.at[v, s, 1], x_recv.at[v, s, PIECES])
            wait_for(outb.at[s], x_send.at[s])

        for c in range(PIECES):
            for t in range(c * kc // TILE, (c + 1) * kc // TILE):
                part = slice(t * TILE, (t + 1) * TILE)
                value = lax.dot_general(uall[row], xv[part, :], NT, preferred_element_type=F32)
                value = inb[v, s, 0, :, part].astype(F32) + inb[v, s, 1, :, part].astype(F32) - value
                high = value.astype(BF16)
                outb[s, 0, :, part] = high
                outb[s, 1, :, part] = (value - high.astype(F32)).astype(BF16)
            part = slice(c * kc, (c + 1) * kc)
            pltpu.make_async_remote_copy(
                outb.at[s, 0, :, part], inb.at[v + 1, s, 0, :, part], x_send.at[s],
                x_recv.at[v + 1, s, c], device_id={"feat": nxt}, device_id_type=MESH).start()
        pltpu.make_async_remote_copy(
            outb.at[s, 1], inb.at[v + 1, s, 1], x_send.at[s],
            x_recv.at[v + 1, s, PIECES], device_id={"feat": nxt}, device_id_type=MESH).start()

    @pl.loop(0, visits)
    def _(v):
        project(v, 0)

        @pl.when(v > 0)
        def _():
            reduce_y(v - 1, 1)

        reduce_z(v, 0)

        @pl.when(v > 0)
        def _():
            apply(v - 1, 1)

        reduce_y(v, 0)
        project(v, 1)
        apply(v, 0)
        reduce_z(v, 1)

    reduce_y(visits - 1, 1)
    apply(visits - 1, 1)

    incs = pltpu.make_async_copy(uall, inc_hbm, out_sem.at[0])
    incs.start()
    for s in range(CHAINS):
        for c in range(PIECES):
            part = slice(c * kc, (c + 1) * kc)
            wait_for(inb.at[visits, s, 0, :, part], x_recv.at[visits, s, c])
        wait_for(inb.at[visits, s, 1], x_recv.at[visits, s, PIECES])

        @pl.loop(0, rows // 128)
        def _(i):
            part = pl.ds(pl.multiple_of(i * 128, 128), 128)
            value = inb[visits, s, 0, :, part].astype(F32) + inb[visits, s, 1, :, part].astype(F32)
            fin[s * width:(s + 1) * width, part] = value

    final = pltpu.make_async_copy(fin, res_hbm, out_sem.at[1])
    final.start()
    for s in range(CHAINS):
        wait_for(outb.at[s], x_send.at[s])
    incs.wait()
    final.wait()


def on_device(nf, nr, features, residual, inverse_grams):
    rows, fb = features.shape
    labels = residual.shape[1]
    nz = nr // NY
    width = labels // CHAINS
    cw = fb // nz
    dma = pltpu.SemaphoreType.DMA
    hbm = pl.BlockSpec(memory_space=pl.ANY)
    increments, final = pl.pallas_call(
        functools.partial(sweep, nf, nz),
        out_shape=(
            jax.ShapeDtypeStruct((nf * CHAINS, width, fb), BF16),
            jax.ShapeDtypeStruct((labels, rows), F32),
        ),
        in_specs=[hbm, hbm, hbm],
        out_specs=(hbm, hbm),
        scratch_shapes=[
            pltpu.VMEM((rows, fb), BF16),
            pltpu.VMEM((rows, fb), BF16),
            pltpu.VMEM((fb, fb), F32),
            pltpu.VMEM((2, fb, fb), BF16),
            pltpu.VMEM((rows, labels), F32),
            pltpu.VMEM((labels, rows), F32),
            pltpu.VMEM((nf + 1, CHAINS, 2, width, rows), BF16),
            pltpu.VMEM((CHAINS, 2, width, rows), BF16),
            pltpu.VMEM((CHAINS, width, fb), F32),
            pltpu.VMEM((CHAINS, nz, width, cw), BF16),
            pltpu.VMEM((nf, CHAINS, nz - 1, width, cw), BF16),
            pltpu.VMEM((nf, CHAINS, NY, width, cw), F32),
            pltpu.VMEM((nf * CHAINS, width, fb), BF16),
            dma((rows // TILE,)),
            dma,
            dma,
            dma((nf + 1, CHAINS, PIECES + 1)),
            dma((CHAINS,)),
            dma((nf, CHAINS)),
            dma((CHAINS,)),
            dma((nf, CHAINS)),
            dma((CHAINS,)),
            dma((nf, CHAINS)),
            dma((CHAINS,)),
            dma((2,)),
        ],
        compiler_params=pltpu.CompilerParams(
            collective_id=0, has_side_effects=True, vmem_limit_bytes=60 * 1024 * 1024
        ),
        name="sweep",
    )(features, residual, inverse_grams)
    return increments.reshape(nf * labels, fb), final.T


def solution(mesh):
    placed = (P("rows", "feat"), P("rows", "feat"), P("feat", None))
    return jax.shard_map(
        functools.partial(on_device, mesh.shape["feat"], mesh.shape["rows"]),
        mesh=mesh,
        in_specs=placed,
        out_specs=(P(None, "feat"), P("rows", "feat")),
        check_vma=False,
    )
```

```python
import functools

import jax
import jax.numpy as jnp
from jax import lax
from jax.experimental import pallas as pl
from jax.experimental.pallas import tpu as pltpu
from jax.sharding import PartitionSpec as P

NY = 4
SCHEDULE = ("P0", "A1-", "L1-", "U0", "P1", "A0", "L0", "U1")
CHAINS = 2
PIECES = 2
TILE = 256
MESH = pl.DeviceIdType.MESH
BF16, F32 = jnp.bfloat16, jnp.float32
NT = (((1,), (1,)), ((), ()))


def wait_for(ref, sem):
    pltpu.make_async_copy(ref, ref, sem).wait()


def sweep(nf, nz, x_hbm, r_hbm, h_hbm, uall, fin, xv, xt, yv, hst, hsp, rst, inb, home, outb,
          acc, q, pv, rb, x_in, h_in, r_in, x_recv, x_send, e_send, q_recv, q_send,
          g_recv, g_send):
    rows, fb = xv.shape
    width = acc.shape[1]
    sw, cw = q.shape[3], q.shape[4]
    kc = rows // PIECES
    visits = nf
    f = lax.axis_index("feat")
    rid = lax.axis_index("rows")
    z, y = rid // NY, rid % NY
    nxt, prv = (f + 1) % nf, (f + nf - 1) % nf
    x_blocks = rows // TILE
    my_rows = pl.ds(pl.multiple_of(y * sw, sw), sw)
    my_cols = pl.ds(pl.multiple_of(z * cw, cw), cw)

    peers = [(dz, dy) for dz in range(nz) for dy in range(NY) if dz or dy]
    peers.sort(key=lambda p: -(min(p[0], nz - p[0]) + min(p[1], NY - p[1])))

    def place(dz, dy):
        return (z + dz) % nz, (y + dy) % NY

    def device(pz, py):
        return {"rows": pz * NY + py}

    def load_x(t):
        part = pl.ds(t * TILE, TILE)
        return pltpu.make_async_copy(x_hbm.at[part], xv.at[part], x_in.at[t])

    pltpu.make_async_copy(r_hbm, rst, r_in).start()
    for t in range(x_blocks):
        load_x(t).start()
    pltpu.make_async_copy(h_hbm, hst, h_in).start()

    barrier = pltpu.get_barrier_semaphore()
    for peer in [device(*place(*p)) for p in peers] + [{"feat": nxt}, {"feat": prv}]:
        pl.semaphore_signal(barrier, inc=1, device_id=peer, device_id_type=MESH)

    pltpu.make_async_copy(r_hbm, rst, r_in).wait()

    @pl.loop(0, rows // 128)
    def _(i):
        part = pl.ds(pl.multiple_of(i * 128, 128), 128)
        value = rst[part, :].T
        high = value.astype(BF16)
        low = (value - high.astype(F32)).astype(BF16)
        for s in range(CHAINS):
            own = slice(s * width, (s + 1) * width)
            inb[0, s, 0, :, part] = high[own]
            inb[0, s, 1, :, part] = low[own]

    for t in range(x_blocks):
        load_x(t).wait()

    def split_inverse():
        pltpu.make_async_copy(h_hbm, hst, h_in).wait()

        @pl.loop(0, fb // 128)
        def _(i):
            part = pl.ds(pl.multiple_of(i * 128, 128), 128)
            value = hst[part, :]
            high = value.astype(BF16)
            hsp[0, part, :] = high
            hsp[1, part, :] = (value - high.astype(F32)).astype(BF16)

    def times_inverse(value, cols):
        high = jnp.dot(value, hsp[0, :, cols], preferred_element_type=F32)
        return high + jnp.dot(value, hsp[1, :, cols], preferred_element_type=F32)

    def form_y(first, last):
        @pl.loop(first, last)
        def _(t):
            part = pl.ds(pl.multiple_of(t * TILE, TILE), TILE)
            block = xv[part, :]
            for n in range(fb // TILE):
                cols = slice(n * TILE, (n + 1) * TILE)
                yv[part, cols] = times_inverse(block, cols).astype(BF16)

    def project(v, s, start=False):
        for c in range(PIECES):
            part = slice(c * kc, (c + 1) * kc)
            if not start:
                wait_for(inb.at[v, s, 0, :, part], x_recv.at[v, s, c])
            high = inb[v, s, 0, :, part]
            for n in range(fb // TILE):
                cols = slice(n * TILE, (n + 1) * TILE)
                value = jnp.dot(high, (xv if start else yv)[part, cols], preferred_element_type=F32)
                if c > 0:
                    value += acc[s, :, cols]
                if c < PIECES - 1:
                    acc[s, :, cols] = value
                else:
                    for i in range(TILE // cw):
                        for j in range(NY):
                            q[s, j, n * (TILE // cw) + i] = value[j * sw:(j + 1) * sw, i * cw:(i + 1) * cw].astype(BF16)
        for i, p in enumerate(peers):
            pz, py = place(*p)
            pltpu.make_async_remote_copy(
                q.at[s, py, pz], rb.at[v, s, i], q_send.at[s], q_recv.at[v, s],
                device_id=device(pz, py), device_id_type=MESH).start()

    def reduce(v, s, start=False):
        wait_for(rb.at[v, s], q_recv.at[v, s])
        total = q[s, y, z].astype(F32)
        for i in range(len(peers)):
            total += rb[v, s, i].astype(F32)
        row = (f - v + nf) % nf * CHAINS + s
        target = pv.at[s] if start else uall.at[row]
        target[my_rows, my_cols] = total.astype(BF16)
        for p in peers:
            pltpu.make_async_remote_copy(
                target.at[my_rows, my_cols], target.at[my_rows, my_cols], g_send.at[s], g_recv.at[v, s],
                device_id=device(*place(*p)), device_id_type=MESH).start()
        wait_for(rb.at[v, s], q_send.at[s])

    def apply(v, s, start=False, last=False):
        row = (f - v + nf) % nf * CHAINS + s
        wait_for(rb.at[v, s], g_recv.at[v, s])
        if start:
            for n in range(fb // TILE):
                cols = slice(n * TILE, (n + 1) * TILE)
                uall[row, :, cols] = times_inverse(pv[s], cols).astype(BF16)
        else:
            if not last:
                wait_for(inb.at[v, s, 1], x_recv.at[v, s, PIECES])
            wait_for(outb.at[s], x_send.at[s])
        for c in range(PIECES):
            for t in range(c * kc // TILE, (c + 1) * kc // TILE):
                part = slice(t * TILE, (t + 1) * TILE)
                if start:
                    value = lax.dot_general(uall[row], xv[part, :], NT, preferred_element_type=F32)
                else:
                    value = jnp.dot(uall[row], xt[:, part], preferred_element_type=F32)
                if last:
                    outb[s, 0, :, part] = value.astype(BF16)
                    continue
                value = inb[v, s, 0, :, part].astype(F32) + inb[v, s, 1, :, part].astype(F32) - value
                high = value.astype(BF16)
                outb[s, 0, :, part] = high
                outb[s, 1, :, part] = (value - high.astype(F32)).astype(BF16)
            part = slice(c * kc, (c + 1) * kc)
            pltpu.make_async_remote_copy(
                outb.at[s, 0, :, part], home.at[s, :, part] if last else inb.at[v + 1, s, 0, :, part], x_send.at[s],
                x_recv.at[v + (2 if last else 1), s, c], device_id={"feat": nxt}, device_id_type=MESH).start()
        wait_for(rb.at[v, s], g_send.at[s])

    def send_low(v, s):
        pltpu.make_async_remote_copy(
            outb.at[s, 1], inb.at[v + 1, s, 1], x_send.at[s],
            x_recv.at[v + 1, s, PIECES], device_id={"feat": nxt}, device_id_type=MESH).start()

    def forward(v, s, i):
        if i == 1:
            wait_for(inb.at[v, s, 1], x_recv.at[v, s, PIECES])
        return pltpu.make_async_remote_copy(
            inb.at[v, s, i], inb.at[v + 1, s, i], e_send.at[s, i],
            x_recv.at[v + 1, s, PIECES if i else 0], device_id={"feat": nxt}, device_id_type=MESH)

    pl.semaphore_wait(barrier, len(peers) + 2)
    for s in range(CHAINS):
        project(0, s, True)
    split_inverse()
    form_y(0, x_blocks // 2)
    for s in range(CHAINS):
        reduce(0, s, True)
    form_y(x_blocks // 2, x_blocks)
    for s in range(CHAINS):
        apply(0, s, True)
    for s in range(CHAINS):
        send_low(0, s)

    @pl.loop(0, rows // 128)
    def _(i):
        part = pl.ds(pl.multiple_of(i * 128, 128), 128)
        xt[:, part] = xv[part, :].T

    stages = {"P": project, "U": reduce, "A": apply, "L": send_low}
    steps = [(stages[w[0]], int(w[1]), len(w) > 2) for w in SCHEDULE]

    @pl.loop(1, visits - 1)
    def _(v):
        for stage, s, late in steps:
            if late:
                @pl.when(v > 1)
                def _():
                    stage(v - 1, s)
            else:
                stage(v, s)

    end = visits - 1
    for stage, s, late in steps:
        if late:
            if end > 1:
                stage(end - 1, s)
            continue
        if stage is send_low:
            continue
        if stage is apply:
            apply(end, s, last=True)
            continue
        stage(end, s)
        if stage is project:
            forward(end, s, 0).start()
        if stage is reduce:
            forward(end, s, 1).start()
    for stage, s, late in steps:
        if late and stage is apply:
            apply(end, s, last=True)

    for s in range(CHAINS):
        wait_for(inb.at[visits, s, 0], x_recv.at[visits, s, 0])
        wait_for(inb.at[visits, s, 1], x_recv.at[visits, s, PIECES])
        for c in range(PIECES):
            part = slice(c * kc, (c + 1) * kc)
            wait_for(home.at[s, :, part], x_recv.at[visits + 1, s, c])

            @pl.loop(c * kc // 128, (c + 1) * kc // 128)
            def _(i):
                part = pl.ds(pl.multiple_of(i * 128, 128), 128)
                value = inb[visits, s, 0, :, part].astype(F32) + inb[visits, s, 1, :, part].astype(F32)
                fin[part, s * width:(s + 1) * width] = (value - home[s, :, part].astype(F32)).T

    for s in range(CHAINS):
        wait_for(inb.at[visits, s, 0], e_send.at[s, 0])
        wait_for(inb.at[visits, s, 1], e_send.at[s, 1])
        wait_for(outb.at[s, 0], x_send.at[s])


def on_device(nf, nr, features, residual, inverse_grams):
    rows, fb = features.shape
    labels = residual.shape[1]
    nz = nr // NY
    width = labels // CHAINS
    cw, sw = fb // nz, width // NY
    dma = pltpu.SemaphoreType.DMA
    hbm = pl.BlockSpec(memory_space=pltpu.HBM)
    vmem = pl.BlockSpec(memory_space=pltpu.VMEM)
    increments, final = pl.pallas_call(
        functools.partial(sweep, nf, nz),
        out_shape=(
            pltpu.VMEM((nf * CHAINS, width, fb), BF16),
            pltpu.VMEM((rows, labels), F32),
        ),
        in_specs=[hbm, hbm, hbm],
        out_specs=(vmem, vmem),
        scratch_shapes=[
            pltpu.VMEM((rows, fb), BF16),
            pltpu.VMEM((fb, rows), BF16),
            pltpu.VMEM((rows, fb), BF16),
            pltpu.VMEM((fb, fb), F32),
            pltpu.VMEM((2, fb, fb), BF16),
            pltpu.VMEM((rows, labels), F32),
            pltpu.VMEM((nf + 1, CHAINS, 2, width, rows), BF16),
            pltpu.VMEM((CHAINS, width, rows), BF16),
            pltpu.VMEM((CHAINS, 2, width, rows), BF16),
            pltpu.VMEM((CHAINS, width, fb), F32),
            pltpu.VMEM((CHAINS, NY, nz, sw, cw), BF16),
            pltpu.VMEM((CHAINS, width, fb), BF16),
            pltpu.VMEM((nf, CHAINS, nr - 1, sw, cw), BF16),
            dma((rows // TILE,)),
            dma,
            dma,
            dma((nf + 2, CHAINS, PIECES + 1)),
            dma((CHAINS,)),
            dma((CHAINS, 2)),
            dma((nf, CHAINS)),
            dma((CHAINS,)),
            dma((nf, CHAINS)),
            dma((CHAINS,)),
        ],
        compiler_params=pltpu.CompilerParams(
            collective_id=0, has_side_effects=True, vmem_limit_bytes=60 * 1024 * 1024
        ),
        name="sweep",
    )(features, residual, inverse_grams)
    return increments.reshape(nf * labels, fb), final


def solution(mesh):
    placed = (P("rows", "feat"), P("rows", "feat"), P("feat", None))
    return jax.shard_map(
        functools.partial(on_device, mesh.shape["feat"], mesh.shape["rows"]),
        mesh=mesh,
        in_specs=placed,
        out_specs=(P(None, "feat"), P("rows", "feat")),
        check_vma=False,
    )
```

```python
import functools

import jax
import jax.numpy as jnp
from jax import lax
from jax.experimental import pallas as pl
from jax.experimental.pallas import tpu as pltpu
from jax.sharding import PartitionSpec as P

NY = 4
SCHEDULE = ("P0", "P1", "U0", "U1", "A0", "A1", "L0", "L1")
CHAINS = 2
PIECES = 2
TILE = 256
MESH = pl.DeviceIdType.MESH
BF16, F32 = jnp.bfloat16, jnp.float32
NT = (((1,), (1,)), ((), ()))


def wait_for(ref, sem):
    pltpu.make_async_copy(ref, ref, sem).wait()


def sweep(nf, nz, x_hbm, r_hbm, h_hbm, uall, fin, xv, xt, yv, hst, hsp, rst, inb, home, outb,
          acc, q, pv, rb, x_in, h_in, r_in, x_recv, x_send, e_send, q_recv, q_send,
          g_recv, g_send):
    rows, fb = xv.shape
    width = acc.shape[1]
    sw, cw = q.shape[3], q.shape[4]
    kc = rows // PIECES
    visits = nf
    f = lax.axis_index("feat")
    rid = lax.axis_index("rows")
    z, y = rid // NY, rid % NY
    nxt, prv = (f + 1) % nf, (f + nf - 1) % nf
    x_blocks = rows // TILE
    my_rows = pl.ds(pl.multiple_of(y * sw, sw), sw)
    my_cols = pl.ds(pl.multiple_of(z * cw, cw), cw)

    peers = [(dz, dy) for dz in range(nz) for dy in range(NY) if dz or dy]
    peers.sort(key=lambda p: -(min(p[0], nz - p[0]) + min(p[1], NY - p[1])))

    def place(dz, dy):
        return (z + dz) % nz, (y + dy) % NY

    def device(pz, py):
        return {"rows": pz * NY + py}

    def load_x(t):
        part = pl.ds(t * TILE, TILE)
        return pltpu.make_async_copy(x_hbm.at[part], xv.at[part], x_in.at[t])

    pltpu.make_async_copy(r_hbm, rst, r_in).start()
    for t in range(x_blocks):
        load_x(t).start()
    pltpu.make_async_copy(h_hbm, hst, h_in).start()

    barrier = pltpu.get_barrier_semaphore()
    for peer in [device(*place(*p)) for p in peers] + [{"feat": nxt}, {"feat": prv}]:
        pl.semaphore_signal(barrier, inc=1, device_id=peer, device_id_type=MESH)

    pltpu.make_async_copy(r_hbm, rst, r_in).wait()

    @pl.loop(0, rows // 128)
    def _(i):
        part = pl.ds(pl.multiple_of(i * 128, 128), 128)
        value = rst[part, :].T
        high = value.astype(BF16)
        low = (value - high.astype(F32)).astype(BF16)
        for s in range(CHAINS):
            own = slice(s * width, (s + 1) * width)
            inb[0, s, 0, :, part] = high[own]
            inb[0, s, 1, :, part] = low[own]

    for t in range(x_blocks):
        load_x(t).wait()

    def split_inverse():
        pltpu.make_async_copy(h_hbm, hst, h_in).wait()

        @pl.loop(0, fb // 128)
        def _(i):
            part = pl.ds(pl.multiple_of(i * 128, 128), 128)
            value = hst[part, :]
            high = value.astype(BF16)
            hsp[0, part, :] = high
            hsp[1, part, :] = (value - high.astype(F32)).astype(BF16)

    def times_inverse(value, cols):
        high = jnp.dot(value, hsp[0, :, cols], preferred_element_type=F32)
        return high + jnp.dot(value, hsp[1, :, cols], preferred_element_type=F32)

    def form_y(first, last):
        @pl.loop(first, last)
        def _(t):
            part = pl.ds(pl.multiple_of(t * TILE, TILE), TILE)
            block = xv[part, :]
            for n in range(fb // TILE):
                cols = slice(n * TILE, (n + 1) * TILE)
                yv[part, cols] = times_inverse(block, cols).astype(BF16)

    def project(v, s, start=False):
        for c in range(PIECES):
            part = slice(c * kc, (c + 1) * kc)
            if not start:
                wait_for(inb.at[v, s, 0, :, part], x_recv.at[v, s, c])
            high = inb[v, s, 0, :, part]
            for n in range(fb // TILE):
                cols = slice(n * TILE, (n + 1) * TILE)
                value = jnp.dot(high, (xv if start else yv)[part, cols], preferred_element_type=F32)
                if c > 0:
                    value += acc[s, :, cols]
                if c < PIECES - 1:
                    acc[s, :, cols] = value
                else:
                    for i in range(TILE // cw):
                        for j in range(NY):
                            q[s, j, n * (TILE // cw) + i] = value[j * sw:(j + 1) * sw, i * cw:(i + 1) * cw].astype(BF16)
        if start and s == 0:
            pl.semaphore_wait(barrier, len(peers) + 2)
        for i, p in enumerate(peers):
            pz, py = place(*p)
            pltpu.make_async_remote_copy(
                q.at[s, py, pz], rb.at[v, s, i], q_send.at[s], q_recv.at[v, s],
                device_id=device(pz, py), device_id_type=MESH).start()

    def reduce(v, s, start=False):
        wait_for(rb.at[v, s], q_recv.at[v, s])
        total = q[s, y, z].astype(F32)
        for i in range(len(peers)):
            total += rb[v, s, i].astype(F32)
        row = (f - v + nf) % nf * CHAINS + s
        target = pv.at[s] if start else uall.at[row]
        target[my_rows, my_cols] = total.astype(BF16)
        for p in peers:
            pltpu.make_async_remote_copy(
                target.at[my_rows, my_cols], target.at[my_rows, my_cols], g_send.at[s], g_recv.at[v, s],
                device_id=device(*place(*p)), device_id_type=MESH).start()
        wait_for(rb.at[v, s], q_send.at[s])

    def apply(v, s, start=False, last=False):
        row = (f - v + nf) % nf * CHAINS + s
        wait_for(rb.at[v, s], g_recv.at[v, s])
        if start:
            for n in range(fb // TILE):
                cols = slice(n * TILE, (n + 1) * TILE)
                uall[row, :, cols] = times_inverse(pv[s], cols).astype(BF16)
        else:
            if not last:
                wait_for(inb.at[v, s, 1], x_recv.at[v, s, PIECES])
            wait_for(outb.at[s], x_send.at[s])
        for c in range(PIECES):
            for t in range(c * kc // TILE, (c + 1) * kc // TILE):
                part = slice(t * TILE, (t + 1) * TILE)
                if start:
                    value = lax.dot_general(uall[row], xv[part, :], NT, preferred_element_type=F32)
                else:
                    value = jnp.dot(uall[row], xt[:, part], preferred_element_type=F32)
                if last:
                    outb[s, 0, :, part] = value.astype(BF16)
                    continue
                value = inb[v, s, 0, :, part].astype(F32) + inb[v, s, 1, :, part].astype(F32) - value
                high = value.astype(BF16)
                outb[s, 0, :, part] = high
                outb[s, 1, :, part] = (value - high.astype(F32)).astype(BF16)
            part = slice(c * kc, (c + 1) * kc)
            pltpu.make_async_remote_copy(
                outb.at[s, 0, :, part], home.at[s, :, part] if last else inb.at[v + 1, s, 0, :, part], x_send.at[s],
                x_recv.at[v + (2 if last else 1), s, c], device_id={"feat": nxt}, device_id_type=MESH).start()
        wait_for(rb.at[v, s], g_send.at[s])

    def send_low(v, s):
        pltpu.make_async_remote_copy(
            outb.at[s, 1], inb.at[v + 1, s, 1], x_send.at[s],
            x_recv.at[v + 1, s, PIECES], device_id={"feat": nxt}, device_id_type=MESH).start()

    def transpose_x():
        @pl.loop(0, rows // 128)
        def _(i):
            part = pl.ds(pl.multiple_of(i * 128, 128), 128)
            xt[:, part] = xv[part, :].T

    def forward(v, s, i):
        if i == 1:
            wait_for(inb.at[v, s, 1], x_recv.at[v, s, PIECES])
        return pltpu.make_async_remote_copy(
            inb.at[v, s, i], inb.at[v + 1, s, i], e_send.at[s, i],
            x_recv.at[v + 1, s, PIECES if i else 0], device_id={"feat": nxt}, device_id_type=MESH)

    for s in range(CHAINS):
        project(0, s, True)
    split_inverse()
    form_y(0, x_blocks // 2)
    for s in range(CHAINS):
        reduce(0, s, True)
    form_y(x_blocks // 2, x_blocks)
    for s in range(CHAINS):
        apply(0, s, True)
    for s in range(CHAINS):
        send_low(0, s)

    stages = {"P": project, "U": reduce, "A": apply, "L": send_low}
    steps = [(stages[w[0]], int(w[1]), len(w) > 2) for w in SCHEDULE]

    middle = [late or stage is not reduce for stage, _, late in steps].index(False)

    @pl.loop(1, visits - 1)
    def _(v):
        for at, (stage, s, late) in enumerate(steps):
            if at == middle:
                pl.when(v == 1)(transpose_x)
            if late:
                @pl.when(v > 1)
                def _():
                    stage(v - 1, s)
            else:
                stage(v, s)

    end = visits - 1
    if end == 1:
        transpose_x()
    for stage, s, late in steps:
        if late:
            if end > 1:
                stage(end - 1, s)
            continue
        if stage is send_low:
            continue
        if stage is apply:
            apply(end, s, last=True)
            continue
        stage(end, s)
        if stage is project:
            forward(end, s, 0).start()
        if stage is reduce:
            forward(end, s, 1).start()
    def finish(s):
        wait_for(inb.at[visits, s, 0], x_recv.at[visits, s, 0])
        wait_for(inb.at[visits, s, 1], x_recv.at[visits, s, PIECES])
        for c in range(PIECES):
            part = slice(c * kc, (c + 1) * kc)
            wait_for(home.at[s, :, part], x_recv.at[visits + 1, s, c])

            @pl.loop(c * kc // 128, (c + 1) * kc // 128)
            def _(i):
                part = pl.ds(pl.multiple_of(i * 128, 128), 128)
                value = inb[visits, s, 0, :, part].astype(F32) + inb[visits, s, 1, :, part].astype(F32)
                fin[part, s * width:(s + 1) * width] = (value - home[s, :, part].astype(F32)).T

    done = []
    for stage, s, late in steps:
        if not late or stage is send_low:
            continue
        if stage is apply:
            finish(s - 1)
            done.append(s - 1)
            apply(end, s, last=True)
        else:
            stage(end, s)
            forward(end, s, 1).start()
    for s in range(CHAINS):
        if s not in done:
            finish(s)

    for s in range(CHAINS):
        wait_for(inb.at[visits, s, 0], e_send.at[s, 0])
        wait_for(inb.at[visits, s, 1], e_send.at[s, 1])
        wait_for(outb.at[s, 0], x_send.at[s])


def on_device(nf, nr, features, residual, inverse_grams):
    rows, fb = features.shape
    labels = residual.shape[1]
    nz = nr // NY
    width = labels // CHAINS
    cw, sw = fb // nz, width // NY
    dma = pltpu.SemaphoreType.DMA
    hbm = pl.BlockSpec(memory_space=pltpu.HBM)
    vmem = pl.BlockSpec(memory_space=pltpu.VMEM)
    increments, final = pl.pallas_call(
        functools.partial(sweep, nf, nz),
        out_shape=(
            pltpu.VMEM((nf * CHAINS, width, fb), BF16),
            pltpu.VMEM((rows, labels), F32),
        ),
        in_specs=[hbm, hbm, hbm],
        out_specs=(vmem, vmem),
        scratch_shapes=[
            pltpu.VMEM((rows, fb), BF16),
            pltpu.VMEM((fb, rows), BF16),
            pltpu.VMEM((rows, fb), BF16),
            pltpu.VMEM((fb, fb), F32),
            pltpu.VMEM((2, fb, fb), BF16),
            pltpu.VMEM((rows, labels), F32),
            pltpu.VMEM((nf + 1, CHAINS, 2, width, rows), BF16),
            pltpu.VMEM((CHAINS, width, rows), BF16),
            pltpu.VMEM((CHAINS, 2, width, rows), BF16),
            pltpu.VMEM((CHAINS, width, fb), F32),
            pltpu.VMEM((CHAINS, NY, nz, sw, cw), BF16),
            pltpu.VMEM((CHAINS, width, fb), BF16),
            pltpu.VMEM((nf, CHAINS, nr - 1, sw, cw), BF16),
            dma((rows // TILE,)),
            dma,
            dma,
            dma((nf + 2, CHAINS, PIECES + 1)),
            dma((CHAINS,)),
            dma((CHAINS, 2)),
            dma((nf, CHAINS)),
            dma((CHAINS,)),
            dma((nf, CHAINS)),
            dma((CHAINS,)),
        ],
        compiler_params=pltpu.CompilerParams(
            collective_id=0, has_side_effects=True, vmem_limit_bytes=60 * 1024 * 1024
        ),
        name="sweep",
    )(features, residual, inverse_grams)
    return increments.reshape(nf * labels, fb), final


def solution(mesh):
    placed = (P("rows", "feat"), P("rows", "feat"), P("feat", None))
    return jax.shard_map(
        functools.partial(on_device, mesh.shape["feat"], mesh.shape["rows"]),
        mesh=mesh,
        in_specs=placed,
        out_specs=(P(None, "feat"), P("rows", "feat")),
        check_vma=False,
    )
```

```python
import functools

import jax
import jax.numpy as jnp
from jax import lax
from jax.experimental import pallas as pl
from jax.experimental.pallas import tpu as pltpu
from jax.sharding import PartitionSpec as P

NY = 4
SCHEDULE = ("P0", "P1", "U0", "U1", "A0", "A1", "L0", "L1")
CHAINS = 2
PIECES = 2
TILE = 512
MESH = pl.DeviceIdType.MESH
BF16, F32 = jnp.bfloat16, jnp.float32
NT = (((1,), (1,)), ((), ()))


def wait_for(ref, sem):
    pltpu.make_async_copy(ref, ref, sem).wait()


def sweep(nf, nz, x_hbm, r_hbm, h_hbm, uall, fin, xv, xt, yv, hst, hsp, rst, inb, home, outb,
          acc, q, pv, rb, x_in, h_in, r_in, x_recv, x_send, e_send, q_recv, q_send,
          g_recv, g_send):
    rows, fb = xv.shape
    width = acc.shape[1]
    sw, cw = q.shape[3], q.shape[4]
    kc = rows // PIECES
    visits = nf
    f = lax.axis_index("feat")
    rid = lax.axis_index("rows")
    z, y = rid // NY, rid % NY
    nxt, prv = (f + 1) % nf, (f + nf - 1) % nf
    x_blocks = rows // TILE
    my_rows = pl.ds(pl.multiple_of(y * sw, sw), sw)
    my_cols = pl.ds(pl.multiple_of(z * cw, cw), cw)

    peers = [(dz, dy) for dz in range(nz) for dy in range(NY) if dz or dy]
    peers.sort(key=lambda p: -(min(p[0], nz - p[0]) + min(p[1], NY - p[1])))

    def place(dz, dy):
        return (z + dz) % nz, (y + dy) % NY

    def device(pz, py):
        return {"rows": pz * NY + py}

    def load_x(t):
        part = pl.ds(t * TILE, TILE)
        return pltpu.make_async_copy(x_hbm.at[part], xv.at[part], x_in.at[t])

    pltpu.make_async_copy(r_hbm, rst, r_in).start()
    for t in range(x_blocks):
        load_x(t).start()
    pltpu.make_async_copy(h_hbm, hst, h_in).start()

    barrier = pltpu.get_barrier_semaphore()
    for peer in [device(*place(*p)) for p in peers] + [{"feat": nxt}, {"feat": prv}]:
        pl.semaphore_signal(barrier, inc=1, device_id=peer, device_id_type=MESH)

    pltpu.make_async_copy(r_hbm, rst, r_in).wait()

    @pl.loop(0, rows // 128)
    def _(i):
        part = pl.ds(pl.multiple_of(i * 128, 128), 128)
        value = rst[part, :].T
        high = value.astype(BF16)
        low = (value - high.astype(F32)).astype(BF16)
        for s in range(CHAINS):
            own = slice(s * width, (s + 1) * width)
            inb[0, s, 0, :, part] = high[own]
            inb[0, s, 1, :, part] = low[own]

    for t in range(x_blocks):
        load_x(t).wait()

    def split_inverse():
        pltpu.make_async_copy(h_hbm, hst, h_in).wait()

        @pl.loop(0, fb // 128)
        def _(i):
            part = pl.ds(pl.multiple_of(i * 128, 128), 128)
            value = hst[part, :]
            high = value.astype(BF16)
            hsp[0, part, :] = high
            hsp[1, part, :] = (value - high.astype(F32)).astype(BF16)

    def times_inverse(value, cols):
        high = jnp.dot(value, hsp[0, :, cols], preferred_element_type=F32)
        return high + jnp.dot(value, hsp[1, :, cols], preferred_element_type=F32)

    def form_y(first, last):
        @pl.loop(first, last)
        def _(t):
            part = pl.ds(pl.multiple_of(t * TILE, TILE), TILE)
            block = xv[part, :]
            for n in range(fb // TILE):
                cols = slice(n * TILE, (n + 1) * TILE)
                yv[part, cols] = times_inverse(block, cols).astype(BF16)

    def project(v, s, start=False):
        for c in range(PIECES):
            part = slice(c * kc, (c + 1) * kc)
            if not start:
                wait_for(inb.at[v, s, 0, :, part], x_recv.at[v, s, c])
            high = inb[v, s, 0, :, part]
            for n in range(fb // TILE):
                cols = slice(n * TILE, (n + 1) * TILE)
                value = jnp.dot(high, (xv if start else yv)[part, cols], preferred_element_type=F32)
                if c > 0:
                    value += acc[s, :, cols]
                if c < PIECES - 1:
                    acc[s, :, cols] = value
                else:
                    for i in range(TILE // cw):
                        for j in range(NY):
                            q[s, j, n * (TILE // cw) + i] = value[j * sw:(j + 1) * sw, i * cw:(i + 1) * cw].astype(BF16)
        if start and s == 0:
            pl.semaphore_wait(barrier, len(peers) + 2)
        for i, p in enumerate(peers):
            pz, py = place(*p)
            pltpu.make_async_remote_copy(
                q.at[s, py, pz], rb.at[v, s, i], q_send.at[s], q_recv.at[v, s],
                device_id=device(pz, py), device_id_type=MESH).start()

    def reduce(v, s, start=False):
        wait_for(rb.at[v, s], q_recv.at[v, s])
        total = q[s, y, z].astype(F32)
        for i in range(len(peers)):
            total += rb[v, s, i].astype(F32)
        row = (f - v + nf) % nf * CHAINS + s
        target = pv.at[s] if start else uall.at[row]
        target[my_rows, my_cols] = total.astype(BF16)
        for p in peers:
            pltpu.make_async_remote_copy(
                target.at[my_rows, my_cols], target.at[my_rows, my_cols], g_send.at[s], g_recv.at[v, s],
                device_id=device(*place(*p)), device_id_type=MESH).start()
        wait_for(rb.at[v, s], q_send.at[s])

    def apply(v, s, start=False, last=False):
        row = (f - v + nf) % nf * CHAINS + s
        wait_for(rb.at[v, s], g_recv.at[v, s])
        if start:
            for n in range(fb // TILE):
                cols = slice(n * TILE, (n + 1) * TILE)
                uall[row, :, cols] = times_inverse(pv[s], cols).astype(BF16)
        else:
            if not last:
                wait_for(inb.at[v, s, 1], x_recv.at[v, s, PIECES])
            wait_for(outb.at[s], x_send.at[s])
        for c in range(PIECES):
            for t in range(c * kc // TILE, (c + 1) * kc // TILE):
                part = slice(t * TILE, (t + 1) * TILE)
                if start:
                    value = lax.dot_general(uall[row], xv[part, :], NT, preferred_element_type=F32)
                else:
                    value = jnp.dot(uall[row], xt[:, part], preferred_element_type=F32)
                if last:
                    outb[s, 0, :, part] = value.astype(BF16)
                    continue
                value = inb[v, s, 0, :, part].astype(F32) + inb[v, s, 1, :, part].astype(F32) - value
                high = value.astype(BF16)
                outb[s, 0, :, part] = high
                outb[s, 1, :, part] = (value - high.astype(F32)).astype(BF16)
            part = slice(c * kc, (c + 1) * kc)
            pltpu.make_async_remote_copy(
                outb.at[s, 0, :, part], home.at[s, :, part] if last else inb.at[v + 1, s, 0, :, part], x_send.at[s],
                x_recv.at[v + (2 if last else 1), s, c], device_id={"feat": nxt}, device_id_type=MESH).start()
        wait_for(rb.at[v, s], g_send.at[s])

    def send_low(v, s):
        pltpu.make_async_remote_copy(
            outb.at[s, 1], inb.at[v + 1, s, 1], x_send.at[s],
            x_recv.at[v + 1, s, PIECES], device_id={"feat": nxt}, device_id_type=MESH).start()

    def transpose_x():
        @pl.loop(0, rows // 128)
        def _(i):
            part = pl.ds(pl.multiple_of(i * 128, 128), 128)
            xt[:, part] = xv[part, :].T

    def forward(v, s, i):
        if i == 1:
            wait_for(inb.at[v, s, 1], x_recv.at[v, s, PIECES])
        return pltpu.make_async_remote_copy(
            inb.at[v, s, i], inb.at[v + 1, s, i], e_send.at[s, i],
            x_recv.at[v + 1, s, PIECES if i else 0], device_id={"feat": nxt}, device_id_type=MESH)

    for s in range(CHAINS):
        project(0, s, True)
    split_inverse()
    form_y(0, x_blocks // 2)
    for s in range(CHAINS):
        reduce(0, s, True)
    form_y(x_blocks // 2, x_blocks)
    for s in range(CHAINS):
        apply(0, s, True)
    for s in range(CHAINS):
        send_low(0, s)

    stages = {"P": project, "U": reduce, "A": apply, "L": send_low}
    steps = [(stages[w[0]], int(w[1]), len(w) > 2) for w in SCHEDULE]

    middle = [late or stage is not reduce for stage, _, late in steps].index(False)

    @pl.loop(1, visits - 1)
    def _(v):
        for at, (stage, s, late) in enumerate(steps):
            if at == middle:
                pl.when(v == 1)(transpose_x)
            if late:
                @pl.when(v > 1)
                def _():
                    stage(v - 1, s)
            else:
                stage(v, s)

    end = visits - 1
    if end == 1:
        transpose_x()
    for stage, s, late in steps:
        if late:
            if end > 1:
                stage(end - 1, s)
            continue
        if stage is send_low:
            continue
        if stage is apply:
            apply(end, s, last=True)
            continue
        stage(end, s)
        if stage is project:
            forward(end, s, 0).start()
        if stage is reduce:
            forward(end, s, 1).start()
    def finish(s):
        wait_for(inb.at[visits, s, 0], x_recv.at[visits, s, 0])
        wait_for(inb.at[visits, s, 1], x_recv.at[visits, s, PIECES])
        for c in range(PIECES):
            part = slice(c * kc, (c + 1) * kc)
            wait_for(home.at[s, :, part], x_recv.at[visits + 1, s, c])

            @pl.loop(c * kc // 128, (c + 1) * kc // 128)
            def _(i):
                part = pl.ds(pl.multiple_of(i * 128, 128), 128)
                value = inb[visits, s, 0, :, part].astype(F32) + inb[visits, s, 1, :, part].astype(F32)
                fin[part, s * width:(s + 1) * width] = (value - home[s, :, part].astype(F32)).T

    done = []
    for stage, s, late in steps:
        if not late or stage is send_low:
            continue
        if stage is apply:
            finish(s - 1)
            done.append(s - 1)
            apply(end, s, last=True)
        else:
            stage(end, s)
            forward(end, s, 1).start()
    for s in range(CHAINS):
        if s not in done:
            finish(s)

    for s in range(CHAINS):
        wait_for(inb.at[visits, s, 0], e_send.at[s, 0])
        wait_for(inb.at[visits, s, 1], e_send.at[s, 1])
        wait_for(outb.at[s, 0], x_send.at[s])


def on_device(nf, nr, features, residual, inverse_grams):
    rows, fb = features.shape
    labels = residual.shape[1]
    nz = nr // NY
    width = labels // CHAINS
    cw, sw = fb // nz, width // NY
    dma = pltpu.SemaphoreType.DMA
    hbm = pl.BlockSpec(memory_space=pltpu.HBM)
    vmem = pl.BlockSpec(memory_space=pltpu.VMEM)
    increments, final = pl.pallas_call(
        functools.partial(sweep, nf, nz),
        out_shape=(
            pltpu.VMEM((nf * CHAINS, width, fb), BF16),
            pltpu.VMEM((rows, labels), F32),
        ),
        in_specs=[hbm, hbm, hbm],
        out_specs=(vmem, vmem),
        scratch_shapes=[
            pltpu.VMEM((rows, fb), BF16),
            pltpu.VMEM((fb, rows), BF16),
            pltpu.VMEM((rows, fb), BF16),
            pltpu.VMEM((fb, fb), F32),
            pltpu.VMEM((2, fb, fb), BF16),
            pltpu.VMEM((rows, labels), F32),
            pltpu.VMEM((nf + 1, CHAINS, 2, width, rows), BF16),
            pltpu.VMEM((CHAINS, width, rows), BF16),
            pltpu.VMEM((CHAINS, 2, width, rows), BF16),
            pltpu.VMEM((CHAINS, width, fb), F32),
            pltpu.VMEM((CHAINS, NY, nz, sw, cw), BF16),
            pltpu.VMEM((CHAINS, width, fb), BF16),
            pltpu.VMEM((nf, CHAINS, nr - 1, sw, cw), BF16),
            dma((rows // TILE,)),
            dma,
            dma,
            dma((nf + 2, CHAINS, PIECES + 1)),
            dma((CHAINS,)),
            dma((CHAINS, 2)),
            dma((nf, CHAINS)),
            dma((CHAINS,)),
            dma((nf, CHAINS)),
            dma((CHAINS,)),
        ],
        compiler_params=pltpu.CompilerParams(
            collective_id=0, has_side_effects=True, vmem_limit_bytes=60 * 1024 * 1024
        ),
        name="sweep",
    )(features, residual, inverse_grams)
    return increments.reshape(nf * labels, fb), final


def solution(mesh):
    placed = (P("rows", "feat"), P("rows", "feat"), P("feat", None))
    return jax.shard_map(
        functools.partial(on_device, mesh.shape["feat"], mesh.shape["rows"]),
        mesh=mesh,
        in_specs=placed,
        out_specs=(P(None, "feat"), P("rows", "feat")),
        check_vma=False,
    )
```
